256 devices in a mesh: dist: 16 (over z_lo, y), rows: 16 (over z_hi, x, core).
Axes of the slice: x: 4, y: 4, z: 8 (z_hi: 2, z_lo: 4; z = z_hi * 4 + z_lo), core: 2. Of those that a mesh axis runs over, the one named last changes fastest.
Arguments:
- wave: float32 [16, 2, 2048, 2048], P('dist', None, 'rows'), may hold values from -6 to 6
- object_slice: float32 [2, 2048, 2048], P(None, 'rows', 'dist'), may hold values from 0 to 1.5
- fresnel: float32 [16], P('dist'), may hold values from 256 to 1024
Outputs:
- detected: float32 [16, 2, 2048, 2048], P('dist', None, 'rows')
The draws below stay inside these ranges and needn't reach their ends.
All inputs are finite; a program needn't handle non-finite values.
Results may differ from the reference program's by a relative error of at most 0.00035.
Values sent between devices are 32-bit elements; how exact they have to be, the bound alone decides.
A program may use at most 64 MiB of HBM per device.

```python
import math
import jax
import jax.numpy as jnp
from jax import lax

N = 2048
DIST = 16


def steps_of(stream_key, dims, split, low, top_value):
    loudness = 1.0
    for dim, shards_of in split:
        draws = jax.random.uniform(jax.random.fold_in(jax.random.fold_in(stream_key, 6), dim), (shards_of,), jnp.float32, low / len(split), top_value / len(split))
        loudness = loudness * jnp.repeat(jnp.exp(draws), dims[dim] // shards_of).reshape((-1,) + (1,) * (len(dims) - 1 - dim))
    return loudness


def scatter_about(own_key, extent, deviation, limit, shards=(), held_as=jnp.bfloat16):
    drawn = jax.random.normal(own_key, extent, jnp.float32) * deviation
    if len(shards) > 0:
        drawn = steps_of(own_key, extent, shards, -0.22, 0.18) * drawn
    return jnp.clip(drawn, min=-limit, max=limit).astype(held_as)


def setup_inputs(seed: int = 0) -> dict:
    splits = jax.random.split(jax.random.key(seed), 4)
    return {
        "wave": scatter_about(splits[0], (DIST, 2, N, N), 1.0, 6.0, ((0, 16), (2, 16)), jnp.float32),
        "object_slice": jnp.clip(1.5 * jax.random.uniform(splits[1], (2, N, N), jnp.float32) ** steps_of(splits[1], (2, N, N), ((1, 16), (2, 16)), -0.2, 0.2), 0.0, 1.5),
        "fresnel": jnp.clip(jnp.exp(math.log(1024.0) - 1.3862944 * jax.random.uniform(splits[2], (DIST,), jnp.float32) ** steps_of(splits[2], (DIST,), ((0, 16),), -0.2, 0.2)), 256.0, 1024.0),
    }


def reference(wave, object_slice, fresnel):
    amplitude = jnp.exp(-object_slice[1])
    trans_re = amplitude * jnp.cos(object_slice[0])
    trans_im = amplitude * jnp.sin(object_slice[0])
    index_line = jnp.arange(N).astype(jnp.int32)
    frequency = jnp.where(index_line < N // 2, index_line, index_line - N).astype(jnp.float32) / N
    freq_sum = frequency[:, None] ** 2 + frequency[None, :] ** 2

    def propagate(inputs):
        field, number = inputs
        exit_re = field[0] * trans_re - field[1] * trans_im
        exit_im = field[0] * trans_im + field[1] * trans_re
        spectrum = jnp.fft.fft2(exit_re + 1j * exit_im)
        phase_angle = (-math.pi * number) * freq_sum
        spectrum = spectrum * (jnp.cos(phase_angle) + 1j * jnp.sin(phase_angle))
        result = jnp.fft.ifft2(spectrum)
        return jnp.stack((jnp.real(result), jnp.imag(result))).astype(jnp.float32)

    return lax.map(propagate, (wave, fresnel))
```

```python
import functools
import math

import jax
import jax.numpy as jnp
from jax import lax
from jax.experimental import pallas as pl
from jax.experimental.pallas import tpu as pltpu
from jax.sharding import PartitionSpec as P

F32 = jnp.float32
BF16 = jnp.bfloat16
LANES = 128
BLOCKS = 16
LENGTH = LANES * BLOCKS
CHUNKS = 4
ROWS = LANES // CHUNKS
SUB = 16


def dft4(points, direction):
    (ar, ai), (br, bi), (cr, ci), (dr, di) = points
    er, ei, fr, fi = ar + cr, ai + ci, ar - cr, ai - ci
    gr, gi, hr, hi = br + dr, bi + di, br - dr, bi - di
    plus, minus = (fr - hi, fi + hr), (fr + hi, fi - hr)
    if direction < 0:
        plus, minus = minus, plus
    return [(er + gr, ei + gi), plus, (er - gr, ei - gi), minus]


def turned(point, steps, direction):
    re, im = point
    steps %= 16
    if steps == 0:
        return point
    if steps == 4:
        return (-im, re) if direction > 0 else (im, -re)
    angle = direction * 2.0 * math.pi * steps / 16
    turn_re, turn_im = math.cos(angle), math.sin(angle)
    if steps == 2:
        return ((re - direction * im) * turn_re, (im + direction * re) * turn_re)
    return (re * turn_re - im * turn_im, re * turn_im + im * turn_re)


def dft16(points, direction):
    inner = [dft4([points[4 * a1 + a0] for a1 in range(4)], direction) for a0 in range(4)]
    out = [None] * 16
    for q0 in range(4):
        column = [turned(inner[a0][q0], a0 * q0, direction) for a0 in range(4)]
        for q1, value in enumerate(dft4(column, direction)):
            out[q0 + 4 * q1] = value
    return out


def halves(value):
    high = value.astype(BF16)
    return high, (value - high.astype(F32)).astype(BF16)


def build_matrices(fresnel, line_ref, s_hi, s_lo):
    q1 = lax.broadcasted_iota(jnp.int32, (BLOCKS, LANES), 0)
    q2 = lax.broadcasted_iota(jnp.int32, (BLOCKS, LANES), 1)
    index = q1 + BLOCKS * q2
    signed = jnp.where(index < LENGTH // 2, index, index - LENGTH).astype(F32)
    turns = fresnel * (signed * signed) * (1.0 / (LENGTH * LENGTH))
    turns = turns - 2.0 * jnp.floor(turns * 0.5 + 0.5)
    phase = -math.pi * turns
    phase_re, phase_im = jnp.cos(phase), jnp.sin(phase)
    row = lax.broadcasted_iota(jnp.int32, (LANES, LANES), 0)
    col = lax.broadcasted_iota(jnp.int32, (LANES, LANES), 1)
    angle = (2.0 * math.pi / LANES) * ((row * col) % LANES).astype(F32)
    table_re, table_im = jnp.cos(angle) * (1.0 / LENGTH), jnp.sin(angle) * (1.0 / LENGTH)
    dot = functools.partial(jnp.dot, precision=lax.Precision.HIGHEST, preferred_element_type=F32)
    line_re = dot(phase_re, table_re) - dot(phase_im, table_im)
    line_im = dot(phase_re, table_im) + dot(phase_im, table_re)
    twist = (2.0 * math.pi / LENGTH) * (q1 * q2).astype(F32)
    twist_re, twist_im = jnp.cos(twist), jnp.sin(twist)
    line_re, line_im = (
        line_re * twist_re - line_im * twist_im,
        line_re * twist_im + line_im * twist_re,
    )
    wrap = (-2.0 * math.pi / BLOCKS) * q1.astype(F32)
    wrap_re, wrap_im = jnp.cos(wrap), jnp.sin(wrap)
    line_ref[0] = line_re
    line_ref[1] = line_im
    line_ref[2] = line_re * wrap_re - line_im * wrap_im
    line_ref[3] = line_re * wrap_im + line_im * wrap_re
    ahead = col >= row

    def one(k, carry):
        def spread(part):
            line = jnp.broadcast_to(line_ref[part, pl.ds(k, 1), :], (LANES, LANES))
            return pltpu.roll(line, 0, 1, stride=1, stride_axis=0)

        re_hi, re_lo = halves(jnp.where(ahead, spread(0), spread(2)))
        im_hi, im_lo = halves(jnp.where(ahead, spread(1), spread(3)))
        for target, re, im in ((s_hi, re_hi, im_hi), (s_lo, re_lo, im_lo)):
            target[k, :LANES, :LANES] = re
            target[k, :LANES, LANES:] = im
            target[k, LANES:, :LANES] = -im
            target[k, LANES:, LANES:] = re
        return carry

    lax.fori_loop(0, BLOCKS, one, 0)


def kernel(
    fresnel_ref, slice_ref, wave_hbm, out_hbm,
    wave, trans, sent, taken, back, line_ref, s_hi, s_lo, lhs, mid, rhs, mid_row,
    wave_sem, z_send, z_recv, y_send, y_recv, go_send, go_recv, back_send, back_recv,
):
    me = lax.axis_index("rows")
    spot = lax.axis_index("dist")
    z_hi, x, core = me // 8, (me // 2) % 4, me % 2
    z_lo, y = spot // 4, spot % 4
    fetch = pltpu.make_async_copy(wave_hbm, wave, wave_sem)
    fetch.start()
    z_peers = [{"dist": (z_lo + k) % 4 * 4 + y, "rows": me} for k in (1, 3, 2)]
    y_peers = [{"dist": z_lo * 4 + (y + k) % 4, "rows": me} for k in (1, 3, 2)]
    row_peers = []
    for far, dx, other in [(f, a, c) for f in (1, 0) for a in (0, 1, 3, 2) for c in (0, 1)]:
        if (far, dx, other) != (0, 0, 0):
            row_peers.append((z_hi + far) % 2 * 8 + (x + dx) % 4 * 2 + (core + other) % 2)

    barrier = pltpu.get_barrier_semaphore()
    peers = z_peers + y_peers + [{"dist": spot, "rows": p} for p in row_peers]
    for peer in peers:
        pl.semaphore_signal(barrier, inc=1, device_id=peer)

    def transmission(g, carry):
        rows = pl.ds(pl.multiple_of(g * ROWS, ROWS), ROWS)
        amplitude = jnp.exp(-slice_ref[1, rows, :])
        trans[g, y, z_lo, 0] = amplitude * jnp.cos(slice_ref[0, rows, :])
        trans[g, y, z_lo, 1] = amplitude * jnp.sin(slice_ref[0, rows, :])
        return carry

    lax.fori_loop(0, CHUNKS, transmission, 0)
    pl.semaphore_wait(barrier, len(peers))

    def z_copies(g):
        own = trans.at[g, y, z_lo]
        return [
            pltpu.make_async_remote_copy(own, own, z_send.at[g], z_recv.at[g], device_id=peer)
            for peer in z_peers
        ]

    def y_copies(g):
        own = trans.at[g, y]
        return [
            pltpu.make_async_remote_copy(own, own, y_send.at[g], y_recv.at[g], device_id=peer)
            for peer in y_peers
        ]

    def z_start(g, carry):
        for copy in z_copies(g):
            copy.start()
        return carry

    lax.fori_loop(0, CHUNKS, z_start, 0)

    def pass_on(g):
        held = trans.at[g, 0, pl.ds(0, 3)]
        pltpu.make_async_copy(held, held, z_recv.at[g]).wait()
        for copy in y_copies(g):
            copy.start()

    pass_on(0)
    build_matrices(fresnel_ref[0], line_ref, s_hi, s_lo)
    fetch.wait()

    def exchange(outbox, target, g, send_sem, recv_sem):
        for p in row_peers:
            pltpu.make_async_remote_copy(
                outbox.at[g, p], target, send_sem.at[g], recv_sem,
                device_id={"dist": spot, "rows": p},
            ).start()
        pltpu.make_async_copy(outbox.at[g, me], target, recv_sem).start()

    def column_part(g, carry):
        @pl.when(g + 1 < CHUNKS)
        def _():
            pass_on(g + 1)

        held = trans.at[g, pl.ds(0, 3)]
        pltpu.make_async_copy(held, held, y_recv.at[g]).wait()

        def forward(j, carry):
            here = pl.ds(pl.multiple_of(j * SUB, SUB), SUB)
            there = pl.ds(pl.multiple_of(g * ROWS + j * SUB, SUB), SUB)
            low = pl.ds(pl.multiple_of(ROWS + j * SUB, SUB), SUB)
            points = []
            for a in range(BLOCKS):
                wave_re = wave[0, there, a * LANES : (a + 1) * LANES]
                wave_im = wave[1, there, a * LANES : (a + 1) * LANES]
                turn_re = trans[g, a % 4, a // 4, 0, here, :]
                turn_im = trans[g, a % 4, a // 4, 1, here, :]
                points.append(
                    (wave_re * turn_re - wave_im * turn_im, wave_re * turn_im + wave_im * turn_re)
                )
            for q, (re, im) in enumerate(dft16(points, -1)):
                re_hi, re_lo = halves(re)
                im_hi, im_lo = halves(im)
                lhs[q, here, :LANES] = re_hi
                lhs[q, here, LANES:] = im_hi
                lhs[q, low, :LANES] = re_lo
                lhs[q, low, LANES:] = im_lo
            return carry

        lax.fori_loop(0, ROWS // SUB, forward, 0)

        def multiply(q, carry):
            both = jnp.dot(lhs[q], s_hi[q], preferred_element_type=F32)
            rest = jnp.dot(lhs[q, :ROWS, :], s_lo[q], preferred_element_type=F32)
            mid[q] = both[:ROWS] + (both[ROWS:] + rest)
            return carry

        lax.fori_loop(0, BLOCKS, multiply, 0, unroll=4)

        def inverse(j, carry):
            here = pl.ds(pl.multiple_of(j * SUB, SUB), SUB)
            points = [(mid[q, here, :LANES], mid[q, here, LANES:]) for q in range(BLOCKS)]
            for a, (re, im) in enumerate(dft16(points, 1)):
                sent[g, a, 0, here, :] = re
                sent[g, a, 1, here, :] = im
            return carry

        lax.fori_loop(0, ROWS // SUB, inverse, 0)
        exchange(sent, taken.at[g, me], g, go_send, go_recv.at[g])
        return carry

    lax.fori_loop(0, CHUNKS, column_part, 0)

    def row_forward(g, carry):
        pltpu.make_async_copy(taken.at[g], taken.at[g], go_recv.at[g]).wait()

        def forward(j, carry):
            here = pl.ds(pl.multiple_of(j * SUB, SUB), SUB)
            re_rows = pl.ds(pl.multiple_of(g * ROWS + j * SUB, SUB), SUB)
            im_rows = pl.ds(pl.multiple_of(LANES + g * ROWS + j * SUB, SUB), SUB)
            points = [(taken[g, a, 0, here, :], taken[g, a, 1, here, :]) for a in range(BLOCKS)]
            for q, (re, im) in enumerate(dft16(points, -1)):
                re_hi, re_lo = halves(re)
                im_hi, im_lo = halves(-im)
                rhs[q, re_rows, :LANES] = re_hi
                rhs[q, re_rows, LANES:] = re_lo
                rhs[q, im_rows, :LANES] = im_hi
                rhs[q, im_rows, LANES:] = im_lo
            return carry

        return lax.fori_loop(0, ROWS // SUB, forward, carry)

    lax.fori_loop(0, CHUNKS, row_forward, 0)

    def row_multiply(q, carry):
        turn = (BLOCKS - q) % BLOCKS
        both = jnp.dot(s_hi[turn], rhs[q], preferred_element_type=F32)
        rest = jnp.dot(s_lo[turn], rhs[q, :, :LANES], preferred_element_type=F32)
        mid_row[q] = both[:, :LANES] + (both[:, LANES:] + rest)
        return carry

    lax.fori_loop(0, BLOCKS, row_multiply, 0, unroll=4)

    def row_inverse(g, carry):
        def inverse(j, carry):
            here = pl.ds(pl.multiple_of(j * SUB, SUB), SUB)
            re_rows = pl.ds(pl.multiple_of(g * ROWS + j * SUB, SUB), SUB)
            im_rows = pl.ds(pl.multiple_of(LANES + g * ROWS + j * SUB, SUB), SUB)
            points = [(mid_row[q, re_rows, :], -mid_row[q, im_rows, :]) for q in range(BLOCKS)]
            for a, (re, im) in enumerate(dft16(points, 1)):
                back[g, a, 0, here, :] = re
                back[g, a, 1, here, :] = im
            return carry

        lax.fori_loop(0, ROWS // SUB, inverse, 0)
        rows = pl.ds(pl.multiple_of(g * ROWS, ROWS), ROWS)
        cols = pl.ds(pl.multiple_of(me * LANES, LANES), LANES)
        exchange(back, out_hbm.at[:, rows, cols], g, back_send, back_recv)
        return carry

    lax.fori_loop(0, CHUNKS, row_inverse, 0)

    def settle(g, carry):
        for copy in z_copies(g):
            copy.wait_send()
        for copy in y_copies(g):
            copy.wait_send()
        some = sent.at[g, pl.ds(0, BLOCKS - 1)]
        pltpu.make_async_copy(some, some, go_send.at[g]).wait()
        pltpu.make_async_copy(some, some, back_send.at[g]).wait()
        return carry

    lax.fori_loop(0, CHUNKS, settle, 0)
    pltpu.make_async_copy(out_hbm, out_hbm, back_recv).wait()


def body(wave, object_slice, fresnel):
    box = (CHUNKS, BLOCKS, 2, ROWS, LANES)
    dma = pltpu.SemaphoreType.DMA
    out = pl.pallas_call(
        kernel,
        out_shape=jax.ShapeDtypeStruct((2, LANES, LENGTH), F32),
        in_specs=[
            pl.BlockSpec(memory_space=pltpu.SMEM),
            pl.BlockSpec(memory_space=pltpu.VMEM),
            pl.BlockSpec(memory_space=pl.ANY),
        ],
        out_specs=pl.BlockSpec(memory_space=pl.ANY),
        scratch_shapes=[
            pltpu.VMEM((2, LANES, LENGTH), F32),
            pltpu.VMEM((CHUNKS, 4, 4, 2, ROWS, LANES), F32),
            pltpu.VMEM(box, F32),
            pltpu.VMEM(box, F32),
            pltpu.VMEM(box, F32),
            pltpu.VMEM((4, BLOCKS, LANES), F32),
            pltpu.VMEM((BLOCKS, 2 * LANES, 2 * LANES), BF16),
            pltpu.VMEM((BLOCKS, 2 * LANES, 2 * LANES), BF16),
            pltpu.VMEM((BLOCKS, 2 * ROWS, 2 * LANES), BF16),
            pltpu.VMEM((BLOCKS, ROWS, 2 * LANES), F32),
            pltpu.VMEM((BLOCKS, 2 * LANES, 2 * LANES), BF16),
            pltpu.VMEM((BLOCKS, 2 * LANES, LANES), F32),
            dma, dma((CHUNKS,)), dma((CHUNKS,)), dma((CHUNKS,)), dma((CHUNKS,)),
            dma((CHUNKS,)), dma((CHUNKS,)), dma((CHUNKS,)), dma,
        ],
        compiler_params=pltpu.CompilerParams(
            collective_id=0, has_side_effects=True, vmem_limit_bytes=48 << 20
        ),
        name="propagate",
    )(fresnel, object_slice, wave[0])
    return out[None]


def solution(mesh):
    return jax.shard_map(
        body,
        mesh=mesh,
        in_specs=(P("dist", None, "rows", None), P(None, "rows", "dist"), P("dist")),
        out_specs=P("dist", None, "rows", None),
        check_vma=False,
    )
```

```python
import functools
import math

import jax
import jax.numpy as jnp
from jax import lax
from jax.experimental import pallas as pl
from jax.experimental.pallas import tpu as pltpu
from jax.sharding import PartitionSpec as P

F32 = jnp.float32
BF16 = jnp.bfloat16
LANES = 128
BLOCKS = 16
LENGTH = LANES * BLOCKS
SUB = 16
GO = ((0, 16), (16, 16), (32, 32), (64, 64))
BACK = ((0, 32), (32, 96))


def dft4(points, direction):
    (ar, ai), (br, bi), (cr, ci), (dr, di) = points
    er, ei, fr, fi = ar + cr, ai + ci, ar - cr, ai - ci
    gr, gi, hr, hi = br + dr, bi + di, br - dr, bi - di
    plus, minus = (fr - hi, fi + hr), (fr + hi, fi - hr)
    if direction < 0:
        plus, minus = minus, plus
    return [(er + gr, ei + gi), plus, (er - gr, ei - gi), minus]


def turned(point, steps, direction):
    re, im = point
    steps %= 16
    if steps == 0:
        return point
    if steps == 4:
        return (-im, re) if direction > 0 else (im, -re)
    angle = direction * 2.0 * math.pi * steps / 16
    turn_re, turn_im = math.cos(angle), math.sin(angle)
    if steps == 2:
        return ((re - direction * im) * turn_re, (im + direction * re) * turn_re)
    return (re * turn_re - im * turn_im, re * turn_im + im * turn_re)


def dft16(points, direction):
    inner = [dft4([points[4 * a1 + a0] for a1 in range(4)], direction) for a0 in range(4)]
    out = [None] * 16
    for q0 in range(4):
        column = [turned(inner[a0][q0], a0 * q0, direction) for a0 in range(4)]
        for q1, value in enumerate(dft4(column, direction)):
            out[q0 + 4 * q1] = value
    return out


def halves(value):
    high = value.astype(BF16)
    return high, (value - high.astype(F32)).astype(BF16)


def build_matrices(fresnel, line_ref, s_hi, s_lo):
    q1 = lax.broadcasted_iota(jnp.int32, (BLOCKS, LANES), 0)
    q2 = lax.broadcasted_iota(jnp.int32, (BLOCKS, LANES), 1)
    index = q1 + BLOCKS * q2
    signed = jnp.where(index < LENGTH // 2, index, index - LENGTH).astype(F32)
    turns = fresnel * (signed * signed) * (1.0 / (LENGTH * LENGTH))
    turns = turns - 2.0 * jnp.floor(turns * 0.5 + 0.5)
    phase = -math.pi * turns
    phase_re, phase_im = jnp.cos(phase), jnp.sin(phase)
    row = lax.broadcasted_iota(jnp.int32, (LANES, LANES), 0)
    col = lax.broadcasted_iota(jnp.int32, (LANES, LANES), 1)
    angle = (2.0 * math.pi / LANES) * ((row * col) % LANES).astype(F32)
    table_re, table_im = jnp.cos(angle) * (1.0 / LENGTH), jnp.sin(angle) * (1.0 / LENGTH)
    dot = functools.partial(jnp.dot, precision=lax.Precision.HIGHEST, preferred_element_type=F32)
    line_re = dot(phase_re, table_re) - dot(phase_im, table_im)
    line_im = dot(phase_re, table_im) + dot(phase_im, table_re)
    twist = (2.0 * math.pi / LENGTH) * (q1 * q2).astype(F32)
    twist_re, twist_im = jnp.cos(twist), jnp.sin(twist)
    line_re, line_im = (
        line_re * twist_re - line_im * twist_im,
        line_re * twist_im + line_im * twist_re,
    )
    wrap = (-2.0 * math.pi / BLOCKS) * q1.astype(F32)
    wrap_re, wrap_im = jnp.cos(wrap), jnp.sin(wrap)
    line_ref[0] = line_re
    line_ref[1] = line_im
    line_ref[2] = line_re * wrap_re - line_im * wrap_im
    line_ref[3] = line_re * wrap_im + line_im * wrap_re
    ahead = col >= row

    def one(k, carry):
        def spread(part):
            line = jnp.broadcast_to(line_ref[part, pl.ds(k, 1), :], (LANES, LANES))
            return pltpu.roll(line, 0, 1, stride=1, stride_axis=0)

        re_hi, re_lo = halves(jnp.where(ahead, spread(0), spread(2)))
        im_hi, im_lo = halves(jnp.where(ahead, spread(1), spread(3)))
        for target, re, im in ((s_hi, re_hi, im_hi), (s_lo, re_lo, im_lo)):
            target[k, :LANES, :LANES] = re
            target[k, :LANES, LANES:] = im
            target[k, LANES:, :LANES] = -im
            target[k, LANES:, LANES:] = re
        return carry

    lax.fori_loop(0, BLOCKS, one, 0)


def kernel(
    fresnel_ref, slice_hbm, wave_hbm, out_hbm,
    piece, wave, trans, sent, taken, back, line_ref, s_hi, s_lo, lhs, mid, rhs, mid_row,
    slice_sem, wave_sem, z_send, z_recv, y_send, y_recv, go_send, go_recv, back_send, back_recv,
):
    me = lax.axis_index("rows")
    spot = lax.axis_index("dist")
    z_hi, x, core = me // 8, (me // 2) % 4, me % 2
    z_lo, y = spot // 4, spot % 4
    fetch_slice = pltpu.make_async_copy(slice_hbm, piece, slice_sem)
    fetch_slice.start()
    fetch = pltpu.make_async_copy(wave_hbm, wave, wave_sem)
    fetch.start()
    z_peers = [{"dist": (z_lo + k) % 4 * 4 + y, "rows": me} for k in (1, 3, 2)]
    y_peers = [{"dist": z_lo * 4 + (y + k) % 4, "rows": me} for k in (1, 3, 2)]
    row_peers = []
    for far, dx, other in [(f, a, c) for f in (1, 0) for a in (0, 1, 3, 2) for c in (0, 1)]:
        if (far, dx, other) != (0, 0, 0):
            row_peers.append((z_hi + far) % 2 * 8 + (x + dx) % 4 * 2 + (core + other) % 2)

    barrier = pltpu.get_barrier_semaphore()
    peers = z_peers + y_peers + [{"dist": spot, "rows": p} for p in row_peers]
    for peer in peers:
        pl.semaphore_signal(barrier, inc=1, device_id=peer)

    fetch_slice.wait()

    def transmission(j, carry):
        rows = pl.ds(pl.multiple_of(j * SUB, SUB), SUB)
        amplitude = jnp.exp(-piece[1, rows, :])
        trans[y, z_lo, 0, rows, :] = amplitude * jnp.cos(piece[0, rows, :])
        trans[y, z_lo, 1, rows, :] = amplitude * jnp.sin(piece[0, rows, :])
        return carry

    lax.fori_loop(0, LANES // SUB, transmission, 0)
    pl.semaphore_wait(barrier, len(peers))

    def z_copies(g):
        own = trans.at[y, z_lo, :, pl.ds(*GO[g])]
        return [
            pltpu.make_async_remote_copy(own, own, z_send.at[g], z_recv.at[g], device_id=peer)
            for peer in z_peers
        ]

    def y_copies(g):
        own = trans.at[y, :, :, pl.ds(*GO[g])]
        return [
            pltpu.make_async_remote_copy(own, own, y_send.at[g], y_recv.at[g], device_id=peer)
            for peer in y_peers
        ]

    def settled(view, sem):
        pltpu.make_async_copy(view, view, sem).wait()

    def pass_on(g):
        settled(trans.at[0, pl.ds(0, 3), :, pl.ds(*GO[g])], z_recv.at[g])
        for copy in y_copies(g):
            copy.start()

    def exchange(outbox, rows, target, send_sem, recv_sem):
        for p in row_peers:
            pltpu.make_async_remote_copy(
                outbox.at[p, :, rows], target, send_sem, recv_sem,
                device_id={"dist": spot, "rows": p},
            ).start()
        pltpu.make_async_copy(outbox.at[me, :, rows], target, recv_sem).start()

    def column_part(first, count):
        def forward(j, carry):
            here = pl.ds(pl.multiple_of(j * SUB, SUB), SUB)
            low = pl.ds(pl.multiple_of(count + j * SUB, SUB), SUB)
            there = pl.ds(pl.multiple_of(first + j * SUB, SUB), SUB)
            points = []
            for a in range(BLOCKS):
                wave_re = wave[0, there, a * LANES : (a + 1) * LANES]
                wave_im = wave[1, there, a * LANES : (a + 1) * LANES]
                turn_re = trans[a % 4, a // 4, 0, there, :]
                turn_im = trans[a % 4, a // 4, 1, there, :]
                points.append(
                    (wave_re * turn_re - wave_im * turn_im, wave_re * turn_im + wave_im * turn_re)
                )
            for q, (re, im) in enumerate(dft16(points, -1)):
                re_hi, re_lo = halves(re)
                im_hi, im_lo = halves(im)
                lhs[q, here, :LANES] = re_hi
                lhs[q, here, LANES:] = im_hi
                lhs[q, low, :LANES] = re_lo
                lhs[q, low, LANES:] = im_lo
            return carry

        lax.fori_loop(0, count // SUB, forward, 0)

        def multiply(q, carry):
            both = jnp.dot(lhs[q, : 2 * count, :], s_hi[q], preferred_element_type=F32)
            rest = jnp.dot(lhs[q, :count, :], s_lo[q], preferred_element_type=F32)
            mid[q, :count, :] = both[:count] + (both[count:] + rest)
            return carry

        lax.fori_loop(0, BLOCKS, multiply, 0, unroll=4)

        def inverse(j, carry):
            here = pl.ds(pl.multiple_of(j * SUB, SUB), SUB)
            there = pl.ds(pl.multiple_of(first + j * SUB, SUB), SUB)
            points = [(mid[q, here, :LANES], mid[q, here, LANES:]) for q in range(BLOCKS)]
            for a, (re, im) in enumerate(dft16(points, 1)):
                sent[a, 0, there, :] = re
                sent[a, 1, there, :] = im
            return carry

        lax.fori_loop(0, count // SUB, inverse, 0)

    for g in range(len(GO)):
        for copy in z_copies(g):
            copy.start()
    for g in range(len(GO)):
        pass_on(g)
    build_matrices(fresnel_ref[0], line_ref, s_hi, s_lo)
    fetch.wait()
    for g, (first, count) in enumerate(GO):
        rows = pl.ds(first, count)
        settled(trans.at[pl.ds(0, 3), :, :, rows], y_recv.at[g])
        column_part(first, count)
        exchange(sent, rows, taken.at[me, :, rows], go_send.at[g], go_recv.at[g])

    def row_forward(j, carry):
        here = pl.ds(pl.multiple_of(j * SUB, SUB), SUB)
        im_rows = pl.ds(pl.multiple_of(LANES + j * SUB, SUB), SUB)
        points = [(taken[a, 0, here, :], taken[a, 1, here, :]) for a in range(BLOCKS)]
        for q, (re, im) in enumerate(dft16(points, -1)):
            re_hi, re_lo = halves(re)
            im_hi, im_lo = halves(-im)
            rhs[q, here, :LANES] = re_hi
            rhs[q, here, LANES:] = re_lo
            rhs[q, im_rows, :LANES] = im_hi
            rhs[q, im_rows, LANES:] = im_lo
        return carry

    for g, (first, count) in enumerate(GO):
        settled(taken.at[:, :, pl.ds(first, count)], go_recv.at[g])
        lax.fori_loop(first // SUB, (first + count) // SUB, row_forward, 0)

    def row_multiply(q, carry):
        turn = (BLOCKS - q) % BLOCKS
        both = jnp.dot(s_hi[turn], rhs[q], preferred_element_type=F32)
        rest = jnp.dot(s_lo[turn], rhs[q, :, :LANES], preferred_element_type=F32)
        mid_row[q] = both[:, :LANES] + (both[:, LANES:] + rest)
        return carry

    lax.fori_loop(0, BLOCKS, row_multiply, 0, unroll=4)

    def row_inverse(j, carry):
        here = pl.ds(pl.multiple_of(j * SUB, SUB), SUB)
        im_rows = pl.ds(pl.multiple_of(LANES + j * SUB, SUB), SUB)
        points = [(mid_row[q, here, :], -mid_row[q, im_rows, :]) for q in range(BLOCKS)]
        for a, (re, im) in enumerate(dft16(points, 1)):
            back[a, 0, here, :] = re
            back[a, 1, here, :] = im
        return carry

    cols = pl.ds(pl.multiple_of(me * LANES, LANES), LANES)
    for g, (first, count) in enumerate(BACK):
        lax.fori_loop(first // SUB, (first + count) // SUB, row_inverse, 0)
        rows = pl.ds(first, count)
        exchange(back, rows, out_hbm.at[:, rows, cols], back_send.at[g], back_recv)

    for g, (first, count) in enumerate(GO):
        for copy in z_copies(g) + y_copies(g):
            copy.wait_send()
        settled(sent.at[pl.ds(0, BLOCKS - 1), :, pl.ds(first, count)], go_send.at[g])
    for g, (first, count) in enumerate(BACK):
        settled(back.at[pl.ds(0, BLOCKS - 1), :, pl.ds(first, count)], back_send.at[g])
    settled(out_hbm, back_recv)


def body(wave, object_slice, fresnel):
    box = pltpu.VMEM((BLOCKS, 2, LANES, LANES), F32)
    matrices = pltpu.VMEM((BLOCKS, 2 * LANES, 2 * LANES), BF16)
    most = max(count for _, count in GO)
    dma = pltpu.SemaphoreType.DMA
    go = dma((len(GO),))
    out = pl.pallas_call(
        kernel,
        out_shape=jax.ShapeDtypeStruct((2, LANES, LENGTH), F32),
        in_specs=[
            pl.BlockSpec(memory_space=pltpu.SMEM),
            pl.BlockSpec(memory_space=pl.ANY),
            pl.BlockSpec(memory_space=pl.ANY),
        ],
        out_specs=pl.BlockSpec(memory_space=pl.ANY),
        scratch_shapes=[
            pltpu.VMEM((2, LANES, LANES), F32),
            pltpu.VMEM((2, LANES, LENGTH), F32),
            pltpu.VMEM((4, 4, 2, LANES, LANES), F32),
            box, box, box,
            pltpu.VMEM((4, BLOCKS, LANES), F32),
            matrices, matrices,
            pltpu.VMEM((BLOCKS, 2 * most, 2 * LANES), BF16),
            pltpu.VMEM((BLOCKS, most, 2 * LANES), F32),
            matrices,
            pltpu.VMEM((BLOCKS, 2 * LANES, LANES), F32),
            dma, dma, go, go, go, go, go, go, dma((len(BACK),)), dma,
        ],
        compiler_params=pltpu.CompilerParams(
            collective_id=0, has_side_effects=True, vmem_limit_bytes=60 << 20
        ),
        name="propagate",
    )(fresnel, object_slice, wave[0])
    return out[None]


def solution(mesh):
    return jax.shard_map(
        body,
        mesh=mesh,
        in_specs=(P("dist", None, "rows", None), P(None, "rows", "dist"), P("dist")),
        out_specs=P("dist", None, "rows", None),
        check_vma=False,
    )
```

```python
import functools
import math

import jax
import jax.numpy as jnp
from jax import lax
from jax.experimental import pallas as pl
from jax.experimental.pallas import tpu as pltpu
from jax.sharding import PartitionSpec as P

F32 = jnp.float32
BF16 = jnp.bfloat16
LANES = 128
BLOCKS = 16
LENGTH = LANES * BLOCKS
SUB = 16
GO = ((0, 32), (32, 32), (64, 64),)
BACK = ((0, 32), (32, 32), (64, 64),)


def dft4(points, direction):
    (ar, ai), (br, bi), (cr, ci), (dr, di) = points
    er, ei, fr, fi = ar + cr, ai + ci, ar - cr, ai - ci
    gr, gi, hr, hi = br + dr, bi + di, br - dr, bi - di
    plus, minus = (fr - hi, fi + hr), (fr + hi, fi - hr)
    if direction < 0:
        plus, minus = minus, plus
    return [(er + gr, ei + gi), plus, (er - gr, ei - gi), minus]


def turned(point, steps, direction):
    re, im = point
    steps %= 16
    if steps == 0:
        return point
    if steps == 4:
        return (-im, re) if direction > 0 else (im, -re)
    angle = direction * 2.0 * math.pi * steps / 16
    turn_re, turn_im = math.cos(angle), math.sin(angle)
    if steps == 2:
        return ((re - direction * im) * turn_re, (im + direction * re) * turn_re)
    return (re * turn_re - im * turn_im, re * turn_im + im * turn_re)


def dft16(points, direction):
    inner = [dft4([points[4 * a1 + a0] for a1 in range(4)], direction) for a0 in range(4)]
    out = [None] * 16
    for q0 in range(4):
        column = [turned(inner[a0][q0], a0 * q0, direction) for a0 in range(4)]
        for q1, value in enumerate(dft4(column, direction)):
            out[q0 + 4 * q1] = value
    return out


def halves(value):
    high = value.astype(BF16)
    return high, (value - high.astype(F32)).astype(BF16)


def build_matrices(fresnel, line_ref, s_hi, s_lo):
    q1 = lax.broadcasted_iota(jnp.int32, (BLOCKS, LANES), 0)
    q2 = lax.broadcasted_iota(jnp.int32, (BLOCKS, LANES), 1)
    index = q1 + BLOCKS * q2
    signed = jnp.where(index < LENGTH // 2, index, index - LENGTH).astype(F32)
    turns = fresnel * (signed * signed) * (1.0 / (LENGTH * LENGTH))
    turns = turns - 2.0 * jnp.floor(turns * 0.5 + 0.5)
    phase = -math.pi * turns
    phase_re, phase_im = jnp.cos(phase), jnp.sin(phase)
    row = lax.broadcasted_iota(jnp.int32, (LANES, LANES), 0)
    col = lax.broadcasted_iota(jnp.int32, (LANES, LANES), 1)
    angle = (2.0 * math.pi / LANES) * ((row * col) % LANES).astype(F32)
    table_re, table_im = jnp.cos(angle) * (1.0 / LENGTH), jnp.sin(angle) * (1.0 / LENGTH)
    dot = functools.partial(jnp.dot, precision=lax.Precision.HIGHEST, preferred_element_type=F32)
    line_re = dot(phase_re, table_re) - dot(phase_im, table_im)
    line_im = dot(phase_re, table_im) + dot(phase_im, table_re)
    twist = (2.0 * math.pi / LENGTH) * (q1 * q2).astype(F32)
    twist_re, twist_im = jnp.cos(twist), jnp.sin(twist)
    line_re, line_im = (
        line_re * twist_re - line_im * twist_im,
        line_re * twist_im + line_im * twist_re,
    )
    wrap = (-2.0 * math.pi / BLOCKS) * q1.astype(F32)
    wrap_re, wrap_im = jnp.cos(wrap), jnp.sin(wrap)
    line_ref[0] = line_re
    line_ref[1] = line_im
    line_ref[2] = line_re * wrap_re - line_im * wrap_im
    line_ref[3] = line_re * wrap_im + line_im * wrap_re
    ahead = col >= row

    def one(k, carry):
        def spread(part):
            line = jnp.broadcast_to(line_ref[part, pl.ds(k, 1), :], (LANES, LANES))
            return pltpu.roll(line, 0, 1, stride=1, stride_axis=0)

        re_hi, re_lo = halves(jnp.where(ahead, spread(0), spread(2)))
        im_hi, im_lo = halves(jnp.where(ahead, spread(1), spread(3)))
        for target, re, im in ((s_hi, re_hi, im_hi), (s_lo, re_lo, im_lo)):
            target[k, :LANES, :LANES] = re
            target[k, :LANES, LANES:] = im
            target[k, LANES:, :LANES] = -im
            target[k, LANES:, LANES:] = re
        return carry

    lax.fori_loop(0, BLOCKS, one, 0)


def kernel(
    fresnel_ref, piece, wave_hbm, out_hbm,
    wave, trans, sent, taken, back, line_ref, s_hi, s_lo, lhs, mid, rhs, mid_row,
    wave_sem, z_send, z_recv, y_send, y_recv, go_send, go_recv, back_send, back_recv, answer,
):
    me = lax.axis_index("rows")
    spot = lax.axis_index("dist")
    z_hi, x, core = me // 8, (me // 2) % 4, me % 2
    z_lo, y = spot // 4, spot % 4
    fetch = pltpu.make_async_copy(wave_hbm, wave, wave_sem)
    fetch.start()
    z_peers = [{"dist": (z_lo + k) % 4 * 4 + y, "rows": me} for k in (1, 3, 2)]
    y_peers = [{"dist": z_lo * 4 + (y + k) % 4, "rows": me} for k in (1, 3, 2)]
    row_peers = []
    for far, dx, other in [(f, a, c) for f in (1, 0) for a in (0, 1, 3, 2) for c in (0, 1)]:
        if (far, dx, other) != (0, 0, 0):
            row_peers.append((z_hi + far) % 2 * 8 + (x + dx) % 4 * 2 + (core + other) % 2)

    barrier = pltpu.get_barrier_semaphore()
    far_peers = [{"dist": spot, "rows": p} for p in row_peers[:8]]
    peers = z_peers + y_peers + [{"dist": spot, "rows": p} for p in row_peers[8:]]
    for peer in peers:
        pl.semaphore_signal(barrier, inc=1, device_id=peer)

    @pl.when(z_hi == 0)
    def _():
        for peer in far_peers:
            pl.semaphore_signal(barrier, inc=1, device_id=peer)

    def transmission(j, carry):
        rows = pl.ds(pl.multiple_of(j * SUB, SUB), SUB)
        amplitude = jnp.exp(-piece[1, rows, :])
        trans[y, z_lo, 0, rows, :] = amplitude * jnp.cos(piece[0, rows, :])
        trans[y, z_lo, 1, rows, :] = amplitude * jnp.sin(piece[0, rows, :])
        return carry

    lax.fori_loop(0, LANES // SUB, transmission, 0)
    pl.semaphore_wait(barrier, len(peers) + len(far_peers) * z_hi)

    @pl.when(z_hi == 1)
    def _():
        for peer in far_peers:
            pl.semaphore_signal(answer, inc=1, device_id=peer)

    def z_copies(g):
        own = trans.at[y, z_lo, :, pl.ds(*GO[g])]
        return [
            pltpu.make_async_remote_copy(own, own, z_send.at[g], z_recv.at[g], device_id=peer)
            for peer in z_peers
        ]

    def y_copies(g):
        own = trans.at[y, :, :, pl.ds(*GO[g])]
        return [
            pltpu.make_async_remote_copy(own, own, y_send.at[g], y_recv.at[g], device_id=peer)
            for peer in y_peers
        ]

    def settled(view, sem):
        pltpu.make_async_copy(view, view, sem).wait()

    def pass_on(g):
        settled(trans.at[0, pl.ds(0, 3), :, pl.ds(*GO[g])], z_recv.at[g])
        for copy in y_copies(g):
            copy.start()

    def exchange(outbox, rows, target, send_sem, recv_sem):
        for p in row_peers:
            pltpu.make_async_remote_copy(
                outbox.at[p, :, rows], target, send_sem, recv_sem,
                device_id={"dist": spot, "rows": p},
            ).start()
        pltpu.make_async_copy(outbox.at[me, :, rows], target, recv_sem).start()

    def column_part(first, count):
        def forward(j, carry):
            here = pl.ds(pl.multiple_of(j * SUB, SUB), SUB)
            low = pl.ds(pl.multiple_of(count + j * SUB, SUB), SUB)
            there = pl.ds(pl.multiple_of(first + j * SUB, SUB), SUB)
            points = []
            for a in range(BLOCKS):
                wave_re = wave[0, there, a * LANES : (a + 1) * LANES]
                wave_im = wave[1, there, a * LANES : (a + 1) * LANES]
                turn_re = trans[a % 4, a // 4, 0, there, :]
                turn_im = trans[a % 4, a // 4, 1, there, :]
                points.append(
                    (wave_re * turn_re - wave_im * turn_im, wave_re * turn_im + wave_im * turn_re)
                )
            for q, (re, im) in enumerate(dft16(points, -1)):
                re_hi, re_lo = halves(re)
                im_hi, im_lo = halves(im)
                lhs[q, here, :LANES] = re_hi
                lhs[q, here, LANES:] = im_hi
                lhs[q, low, :LANES] = re_lo
                lhs[q, low, LANES:] = im_lo
            return carry

        lax.fori_loop(0, count // SUB, forward, 0)

        def multiply(q, carry):
            both = jnp.dot(lhs[q, : 2 * count, :], s_hi[q], preferred_element_type=F32)
            rest = jnp.dot(lhs[q, :count, :], s_lo[q], preferred_element_type=F32)
            mid[q, :count, :] = both[:count] + (both[count:] + rest)
            return carry

        lax.fori_loop(0, BLOCKS, multiply, 0, unroll=4)

        def inverse(j, carry):
            here = pl.ds(pl.multiple_of(j * SUB, SUB), SUB)
            there = pl.ds(pl.multiple_of(first + j * SUB, SUB), SUB)
            points = [(mid[q, here, :LANES], mid[q, here, LANES:]) for q in range(BLOCKS)]
            for a, (re, im) in enumerate(dft16(points, 1)):
                sent[a, 0, there, :] = re
                sent[a, 1, there, :] = im
            return carry

        lax.fori_loop(0, count // SUB, inverse, 0)

    for g in range(len(GO)):
        for copy in z_copies(g):
            copy.start()
    build_matrices(fresnel_ref[0], line_ref, s_hi, s_lo)
    for g in range(len(GO)):
        pass_on(g)
    fetch.wait()
    for g, (first, count) in enumerate(GO):
        rows = pl.ds(first, count)
        settled(trans.at[pl.ds(0, 3), :, :, rows], y_recv.at[g])
        column_part(first, count)
        if g == 0:

            @pl.when(z_hi == 0)
            def _():
                pl.semaphore_wait(answer, len(far_peers))

        exchange(sent, rows, taken.at[me, :, rows], go_send.at[g], go_recv.at[g])

    def row_forward(j, carry):
        here = pl.ds(pl.multiple_of(j * SUB, SUB), SUB)
        im_rows = pl.ds(pl.multiple_of(LANES + j * SUB, SUB), SUB)
        points = [(taken[a, 0, here, :], taken[a, 1, here, :]) for a in range(BLOCKS)]
        for q, (re, im) in enumerate(dft16(points, -1)):
            re_hi, re_lo = halves(re)
            im_hi, im_lo = halves(-im)
            rhs[q, here, :LANES] = re_hi
            rhs[q, here, LANES:] = re_lo
            rhs[q, im_rows, :LANES] = im_hi
            rhs[q, im_rows, LANES:] = im_lo
        return carry

    for g, (first, count) in enumerate(GO):
        settled(taken.at[:, :, pl.ds(first, count)], go_recv.at[g])
        lax.fori_loop(first // SUB, (first + count) // SUB, row_forward, 0)

    def row_multiply(q, carry):
        turn = (BLOCKS - q) % BLOCKS
        both = jnp.dot(s_hi[turn], rhs[q], preferred_element_type=F32)
        rest = jnp.dot(s_lo[turn], rhs[q, :, :LANES], preferred_element_type=F32)
        mid_row[q] = both[:, :LANES] + (both[:, LANES:] + rest)
        return carry

    lax.fori_loop(0, BLOCKS, row_multiply, 0, unroll=4)

    def row_inverse(j, carry):
        here = pl.ds(pl.multiple_of(j * SUB, SUB), SUB)
        im_rows = pl.ds(pl.multiple_of(LANES + j * SUB, SUB), SUB)
        points = [(mid_row[q, here, :], -mid_row[q, im_rows, :]) for q in range(BLOCKS)]
        for a, (re, im) in enumerate(dft16(points, 1)):
            back[a, 0, here, :] = re
            back[a, 1, here, :] = im
        return carry

    cols = pl.ds(pl.multiple_of(me * LANES, LANES), LANES)
    for g, (first, count) in enumerate(BACK):
        lax.fori_loop(first // SUB, (first + count) // SUB, row_inverse, 0)
        rows = pl.ds(first, count)
        exchange(back, rows, out_hbm.at[:, rows, cols], back_send.at[g], back_recv)

    for g, (first, count) in enumerate(GO):
        for copy in z_copies(g) + y_copies(g):
            copy.wait_send()
        settled(sent.at[pl.ds(0, BLOCKS - 1), :, pl.ds(first, count)], go_send.at[g])
    for g, (first, count) in enumerate(BACK):
        settled(back.at[pl.ds(0, BLOCKS - 1), :, pl.ds(first, count)], back_send.at[g])
    settled(out_hbm, back_recv)


def body(wave, object_slice, fresnel):
    box = pltpu.VMEM((BLOCKS, 2, LANES, LANES), F32)
    matrices = pltpu.VMEM((BLOCKS, 2 * LANES, 2 * LANES), BF16)
    most = max(count for _, count in GO)
    dma = pltpu.SemaphoreType.DMA
    go = dma((len(GO),))
    out = pl.pallas_call(
        kernel,
        out_shape=jax.ShapeDtypeStruct((2, LANES, LENGTH), F32),
        in_specs=[
            pl.BlockSpec(memory_space=pltpu.SMEM),
            pl.BlockSpec(memory_space=pltpu.VMEM),
            pl.BlockSpec(memory_space=pl.ANY),
        ],
        out_specs=pl.BlockSpec(memory_space=pl.ANY),
        scratch_shapes=[
            pltpu.VMEM((2, LANES, LENGTH), F32),
            pltpu.VMEM((4, 4, 2, LANES, LANES), F32),
            box, box, box,
            pltpu.VMEM((4, BLOCKS, LANES), F32),
            matrices, matrices,
            pltpu.VMEM((BLOCKS, 2 * most, 2 * LANES), BF16),
            pltpu.VMEM((BLOCKS, most, 2 * LANES), F32),
            matrices,
            pltpu.VMEM((BLOCKS, 2 * LANES, LANES), F32),
            dma, go, go, go, go, go, go, dma((len(BACK),)), dma,
            pltpu.SemaphoreType.REGULAR,
        ],
        compiler_params=pltpu.CompilerParams(
            collective_id=0, has_side_effects=True, vmem_limit_bytes=50 << 20
        ),
        name="propagate",
    )(fresnel, object_slice, wave[0])
    return out[None]


def solution(mesh):
    return jax.shard_map(
        body,
        mesh=mesh,
        in_specs=(P("dist", None, "rows", None), P(None, "rows", "dist"), P("dist")),
        out_specs=P("dist", None, "rows", None),
        check_vma=False,
    )
```

```python
import functools
import math

import jax
import jax.numpy as jnp
from jax import lax
from jax.experimental import pallas as pl
from jax.experimental.pallas import tpu as pltpu
from jax.sharding import PartitionSpec as P

F32 = jnp.float32
BF16 = jnp.bfloat16
LANES = 128
BLOCKS = 16
LENGTH = LANES * BLOCKS
SUB = 16
GO = ((0, 32), (32, 32), (64, 64),)
BACK = ((0, 32), (32, 32), (64, 64),)


def dft4(points, direction):
    (ar, ai), (br, bi), (cr, ci), (dr, di) = points
    er, ei, fr, fi = ar + cr, ai + ci, ar - cr, ai - ci
    gr, gi, hr, hi = br + dr, bi + di, br - dr, bi - di
    plus, minus = (fr - hi, fi + hr), (fr + hi, fi - hr)
    if direction < 0:
        plus, minus = minus, plus
    return [(er + gr, ei + gi), plus, (er - gr, ei - gi), minus]


def turned(point, steps, direction):
    re, im = point
    steps %= 16
    if steps == 0:
        return point
    if steps == 4:
        return (-im, re) if direction > 0 else (im, -re)
    angle = direction * 2.0 * math.pi * steps / 16
    turn_re, turn_im = math.cos(angle), math.sin(angle)
    if steps == 2:
        return ((re - direction * im) * turn_re, (im + direction * re) * turn_re)
    return (re * turn_re - im * turn_im, re * turn_im + im * turn_re)


def dft16(points, direction):
    inner = [dft4([points[4 * a1 + a0] for a1 in range(4)], direction) for a0 in range(4)]
    out = [None] * 16
    for q0 in range(4):
        column = [turned(inner[a0][q0], a0 * q0, direction) for a0 in range(4)]
        for q1, value in enumerate(dft4(column, direction)):
            out[q0 + 4 * q1] = value
    return out


def halves(value):
    high = value.astype(BF16)
    return high, (value - high.astype(F32)).astype(BF16)


def build_matrices(fresnel, line_ref, s_hi, s_lo):
    q1 = lax.broadcasted_iota(jnp.int32, (BLOCKS, LANES), 0)
    q2 = lax.broadcasted_iota(jnp.int32, (BLOCKS, LANES), 1)
    index = q1 + BLOCKS * q2
    signed = jnp.where(index < LENGTH // 2, index, index - LENGTH).astype(F32)
    turns = fresnel * (signed * signed) * (1.0 / (LENGTH * LENGTH))
    turns = turns - 2.0 * jnp.floor(turns * 0.5 + 0.5)
    phase = -math.pi * turns
    phase_re, phase_im = jnp.cos(phase), jnp.sin(phase)
    row = lax.broadcasted_iota(jnp.int32, (LANES, LANES), 0)
    col = lax.broadcasted_iota(jnp.int32, (LANES, LANES), 1)
    angle = (2.0 * math.pi / LANES) * ((row * col) % LANES).astype(F32)
    table_re, table_im = jnp.cos(angle) * (1.0 / LENGTH), jnp.sin(angle) * (1.0 / LENGTH)
    dot = functools.partial(jnp.dot, precision=lax.Precision.HIGHEST, preferred_element_type=F32)
    line_re = dot(phase_re, table_re) - dot(phase_im, table_im)
    line_im = dot(phase_re, table_im) + dot(phase_im, table_re)
    twist = (2.0 * math.pi / LENGTH) * (q1 * q2).astype(F32)
    twist_re, twist_im = jnp.cos(twist), jnp.sin(twist)
    line_re, line_im = (
        line_re * twist_re - line_im * twist_im,
        line_re * twist_im + line_im * twist_re,
    )
    wrap = (-2.0 * math.pi / BLOCKS) * q1.astype(F32)
    wrap_re, wrap_im = jnp.cos(wrap), jnp.sin(wrap)
    line_ref[0] = line_re
    line_ref[1] = line_im
    line_ref[2] = line_re * wrap_re - line_im * wrap_im
    line_ref[3] = line_re * wrap_im + line_im * wrap_re
    ahead = col >= row

    def one(k, carry):
        def spread(part):
            line = jnp.broadcast_to(line_ref[part, pl.ds(k, 1), :], (LANES, LANES))
            return pltpu.roll(line, 0, 1, stride=1, stride_axis=0)

        re_hi, re_lo = halves(jnp.where(ahead, spread(0), spread(2)))
        im_hi, im_lo = halves(jnp.where(ahead, spread(1), spread(3)))
        for target, re, im in ((s_hi, re_hi, im_hi), (s_lo, re_lo, im_lo)):
            target[k, :LANES, :LANES] = re
            target[k, :LANES, LANES:] = im
            target[k, LANES:, :LANES] = -im
            target[k, LANES:, LANES:] = re
        return carry

    lax.fori_loop(0, BLOCKS, one, 0)


def kernel(
    fresnel_ref, slice_hbm, wave_hbm, out_hbm,
    piece, wave, trans, sent, taken, back, line_ref, s_hi, s_lo, lhs, mid, rhs, mid_row,
    slice_sem, wave_sem, z_send, z_recv, y_send, y_recv, go_send, go_recv, back_send, back_recv, answer, ready,
):
    me = lax.axis_index("rows")
    spot = lax.axis_index("dist")
    z_hi, x, core = me // 8, (me // 2) % 4, me % 2
    z_lo, y = spot // 4, spot % 4
    fetch_slice = pltpu.make_async_copy(slice_hbm, piece, slice_sem)
    fetch_slice.start()
    fetch = pltpu.make_async_copy(wave_hbm, wave, wave_sem)
    fetch.start()
    z_peers = [{"dist": (z_lo + k) % 4 * 4 + y, "rows": me} for k in (1, 3, 2)]
    y_peers = [{"dist": z_lo * 4 + (y + k) % 4, "rows": me} for k in (1, 3, 2)]
    row_peers = []
    for far, dx, other in [(f, a, c) for f in (1, 0) for a in (0, 1, 3, 2) for c in (0, 1)]:
        if (far, dx, other) != (0, 0, 0):
            row_peers.append((z_hi + far) % 2 * 8 + (x + dx) % 4 * 2 + (core + other) % 2)

    near_and_far = [p for pair in zip(row_peers[:7], row_peers[8:]) for p in pair] + row_peers[7:8]
    barrier = pltpu.get_barrier_semaphore()
    far_peers = [{"dist": spot, "rows": p} for p in row_peers[:8]]
    peers = z_peers + y_peers + [{"dist": spot, "rows": p} for p in row_peers[8:]]
    for peer in peers:
        pl.semaphore_signal(barrier, inc=1, device_id=peer)

    @pl.when(z_hi == 0)
    def _():
        for peer in far_peers:
            pl.semaphore_signal(barrier, inc=1, device_id=peer)

    fetch_slice.wait()

    def transmission(j, carry):
        rows = pl.ds(pl.multiple_of(j * SUB, SUB), SUB)
        amplitude = jnp.exp(-piece[1, rows, :])
        trans[y, z_lo, 0, rows, :] = amplitude * jnp.cos(piece[0, rows, :])
        trans[y, z_lo, 1, rows, :] = amplitude * jnp.sin(piece[0, rows, :])
        return carry

    lax.fori_loop(0, LANES // SUB, transmission, 0)
    pl.semaphore_wait(barrier, len(peers) + len(far_peers) * z_hi)

    @pl.when(z_hi == 1)
    def _():
        for peer in far_peers:
            pl.semaphore_signal(answer, inc=1, device_id=peer)

    def z_copies(g):
        own = trans.at[y, z_lo, :, pl.ds(*GO[g])]
        return [
            pltpu.make_async_remote_copy(own, own, z_send.at[g], z_recv.at[g], device_id=peer)
            for peer in z_peers
        ]

    def y_copies(g):
        own = trans.at[y, :, :, pl.ds(*GO[g])]
        return [
            pltpu.make_async_remote_copy(own, own, y_send.at[g], y_recv.at[g], device_id=peer)
            for peer in y_peers
        ]

    def settled(view, sem):
        pltpu.make_async_copy(view, view, sem).wait()

    def pass_on(g):
        settled(trans.at[0, pl.ds(0, 3), :, pl.ds(*GO[g])], z_recv.at[g])
        for copy in y_copies(g):
            copy.start()
        if g + 1 == len(GO):
            for peer in z_peers:
                pl.semaphore_signal(ready, inc=1, device_id=peer)

    def exchange(order, outbox, rows, target, send_sem, recv_sem):
        for p in order:
            pltpu.make_async_remote_copy(
                outbox.at[p, :, rows], target, send_sem, recv_sem,
                device_id={"dist": spot, "rows": p},
            ).start()
        pltpu.make_async_copy(outbox.at[me, :, rows], target, recv_sem).start()

    def column_part(first, count):
        def forward(j, carry):
            here = pl.ds(pl.multiple_of(j * SUB, SUB), SUB)
            low = pl.ds(pl.multiple_of(count + j * SUB, SUB), SUB)
            there = pl.ds(pl.multiple_of(first + j * SUB, SUB), SUB)
            points = []
            for a in range(BLOCKS):
                wave_re = wave[0, there, a * LANES : (a + 1) * LANES]
                wave_im = wave[1, there, a * LANES : (a + 1) * LANES]
                turn_re = trans[a % 4, a // 4, 0, there, :]
                turn_im = trans[a % 4, a // 4, 1, there, :]
                points.append(
                    (wave_re * turn_re - wave_im * turn_im, wave_re * turn_im + wave_im * turn_re)
                )
            for q, (re, im) in enumerate(dft16(points, -1)):
                re_hi, re_lo = halves(re)
                im_hi, im_lo = halves(im)
                lhs[q, here, :LANES] = re_hi
                lhs[q, here, LANES:] = im_hi
                lhs[q, low, :LANES] = re_lo
                lhs[q, low, LANES:] = im_lo
            return carry

        lax.fori_loop(0, count // SUB, forward, 0)

        def multiply(q, carry):
            both = jnp.dot(lhs[q, : 2 * count, :], s_hi[q], preferred_element_type=F32)
            rest = jnp.dot(lhs[q, :count, :], s_lo[q], preferred_element_type=F32)
            mid[q, :count, :] = both[:count] + (both[count:] + rest)
            return carry

        lax.fori_loop(0, BLOCKS, multiply, 0, unroll=4)

        def inverse(j, carry):
            here = pl.ds(pl.multiple_of(j * SUB, SUB), SUB)
            there = pl.ds(pl.multiple_of(first + j * SUB, SUB), SUB)
            points = [(mid[q, here, :LANES], mid[q, here, LANES:]) for q in range(BLOCKS)]
            for a, (re, im) in enumerate(dft16(points, 1)):
                sent[a, 0, there, :] = re
                sent[a, 1, there, :] = im
            return carry

        lax.fori_loop(0, count // SUB, inverse, 0)

    for g in range(len(GO)):
        for copy in z_copies(g):
            copy.start()
    build_matrices(fresnel_ref[0], line_ref, s_hi, s_lo)
    for g in range(len(GO)):
        pass_on(g)
    fetch.wait()
    for g, (first, count) in enumerate(GO):
        rows = pl.ds(first, count)
        settled(trans.at[pl.ds(0, 3), :, :, rows], y_recv.at[g])
        column_part(first, count)
        if g == 0:
            pl.semaphore_wait(ready, len(z_peers))

            @pl.when(z_hi == 0)
            def _():
                pl.semaphore_wait(answer, len(far_peers))

        exchange(near_and_far, sent, rows, taken.at[me, :, rows], go_send.at[g], go_recv.at[g])

    def row_forward(j, carry):
        here = pl.ds(pl.multiple_of(j * SUB, SUB), SUB)
        im_rows = pl.ds(pl.multiple_of(LANES + j * SUB, SUB), SUB)
        points = [(taken[a, 0, here, :], taken[a, 1, here, :]) for a in range(BLOCKS)]
        for q, (re, im) in enumerate(dft16(points, -1)):
            re_hi, re_lo = halves(re)
            im_hi, im_lo = halves(-im)
            rhs[q, here, :LANES] = re_hi
            rhs[q, here, LANES:] = re_lo
            rhs[q, im_rows, :LANES] = im_hi
            rhs[q, im_rows, LANES:] = im_lo
        return carry

    for g, (first, count) in enumerate(GO):
        settled(taken.at[:, :, pl.ds(first, count)], go_recv.at[g])
        lax.fori_loop(first // SUB, (first + count) // SUB, row_forward, 0)

    def row_multiply(q, carry):
        turn = (BLOCKS - q) % BLOCKS
        both = jnp.dot(s_hi[turn], rhs[q], preferred_element_type=F32)
        rest = jnp.dot(s_lo[turn], rhs[q, :, :LANES], preferred_element_type=F32)
        mid_row[q] = both[:, :LANES] + (both[:, LANES:] + rest)
        return carry

    lax.fori_loop(0, BLOCKS, row_multiply, 0, unroll=4)

    def row_inverse(j, carry):
        here = pl.ds(pl.multiple_of(j * SUB, SUB), SUB)
        im_rows = pl.ds(pl.multiple_of(LANES + j * SUB, SUB), SUB)
        points = [(mid_row[q, here, :], -mid_row[q, im_rows, :]) for q in range(BLOCKS)]
        for a, (re, im) in enumerate(dft16(points, 1)):
            back[a, 0, here, :] = re
            back[a, 1, here, :] = im
        return carry

    cols = pl.ds(pl.multiple_of(me * LANES, LANES), LANES)
    for g, (first, count) in enumerate(BACK):
        lax.fori_loop(first // SUB, (first + count) // SUB, row_inverse, 0)
        rows = pl.ds(first, count)
        exchange(row_peers, back, rows, out_hbm.at[:, rows, cols], back_send.at[g], back_recv)

    for g, (first, count) in enumerate(GO):
        for copy in z_copies(g) + y_copies(g):
            copy.wait_send()
        settled(sent.at[pl.ds(0, BLOCKS - 1), :, pl.ds(first, count)], go_send.at[g])
    for g, (first, count) in enumerate(BACK):
        settled(back.at[pl.ds(0, BLOCKS - 1), :, pl.ds(first, count)], back_send.at[g])
    settled(out_hbm, back_recv)


def body(wave, object_slice, fresnel):
    box = pltpu.VMEM((BLOCKS, 2, LANES, LANES), F32)
    matrices = pltpu.VMEM((BLOCKS, 2 * LANES, 2 * LANES), BF16)
    most = max(count for _, count in GO)
    dma = pltpu.SemaphoreType.DMA
    go = dma((len(GO),))
    out = pl.pallas_call(
        kernel,
        out_shape=jax.ShapeDtypeStruct((2, LANES, LENGTH), F32),
        in_specs=[
            pl.BlockSpec(memory_space=pltpu.SMEM),
            pl.BlockSpec(memory_space=pl.ANY),
            pl.BlockSpec(memory_space=pl.ANY),
        ],
        out_specs=pl.BlockSpec(memory_space=pl.ANY),
        scratch_shapes=[
            pltpu.VMEM((2, LANES, LANES), F32),
            pltpu.VMEM((2, LANES, LENGTH), F32),
            pltpu.VMEM((4, 4, 2, LANES, LANES), F32),
            box, box, box,
            pltpu.VMEM((4, BLOCKS, LANES), F32),
            matrices, matrices,
            pltpu.VMEM((BLOCKS, 2 * most, 2 * LANES), BF16),
            pltpu.VMEM((BLOCKS, most, 2 * LANES), F32),
            matrices,
            pltpu.VMEM((BLOCKS, 2 * LANES, LANES), F32),
            dma, dma, go, go, go, go, go, go, dma((len(BACK),)), dma,
            pltpu.SemaphoreType.REGULAR, pltpu.SemaphoreType.REGULAR,
        ],
        compiler_params=pltpu.CompilerParams(
            collective_id=0, has_side_effects=True, vmem_limit_bytes=50 << 20
        ),
        name="propagate",
    )(fresnel, *(pltpu.with_memory_space_constraint(a, pltpu.HBM) for a in (object_slice, wave[0])))
    return out[None]


def solution(mesh):
    return jax.shard_map(
        body,
        mesh=mesh,
        in_specs=(P("dist", None, "rows", None), P(None, "rows", "dist"), P("dist")),
        out_specs=P("dist", None, "rows", None),
        check_vma=False,
    )
```

```python
import functools
import math

import jax
import jax.numpy as jnp
from jax import lax
from jax.experimental import pallas as pl
from jax.experimental.pallas import tpu as pltpu
from jax.sharding import PartitionSpec as P

F32 = jnp.float32
BF16 = jnp.bfloat16
LANES = 128
BLOCKS = 16
LENGTH = LANES * BLOCKS
SUB = 16
GO = ((0, 32), (32, 32), (64, 64),)
BACK = ((0, 32), (32, 32), (64, 64),)


def dft4(points, direction):
    (ar, ai), (br, bi), (cr, ci), (dr, di) = points
    er, ei, fr, fi = ar + cr, ai + ci, ar - cr, ai - ci
    gr, gi, hr, hi = br + dr, bi + di, br - dr, bi - di
    plus, minus = (fr - hi, fi + hr), (fr + hi, fi - hr)
    if direction < 0:
        plus, minus = minus, plus
    return [(er + gr, ei + gi), plus, (er - gr, ei - gi), minus]


def turned(point, steps, direction):
    re, im = point
    steps %= 16
    if steps == 0:
        return point
    if steps == 4:
        return (-im, re) if direction > 0 else (im, -re)
    angle = direction * 2.0 * math.pi * steps / 16
    turn_re, turn_im = math.cos(angle), math.sin(angle)
    if steps == 2:
        return ((re - direction * im) * turn_re, (im + direction * re) * turn_re)
    return (re * turn_re - im * turn_im, re * turn_im + im * turn_re)


def dft16(points, direction):
    inner = [dft4([points[4 * a1 + a0] for a1 in range(4)], direction) for a0 in range(4)]
    out = [None] * 16
    for q0 in range(4):
        column = [turned(inner[a0][q0], a0 * q0, direction) for a0 in range(4)]
        for q1, value in enumerate(dft4(column, direction)):
            out[q0 + 4 * q1] = value
    return out


def halves(value):
    high = value.astype(BF16)
    return high, (value - high.astype(F32)).astype(BF16)


def build_matrices(fresnel, line_ref, s_hi, s_lo):
    q1 = lax.broadcasted_iota(jnp.int32, (BLOCKS, LANES), 0)
    q2 = lax.broadcasted_iota(jnp.int32, (BLOCKS, LANES), 1)
    index = q1 + BLOCKS * q2
    signed = jnp.where(index < LENGTH // 2, index, index - LENGTH).astype(F32)
    turns = fresnel * (signed * signed) * (1.0 / (LENGTH * LENGTH))
    turns = turns - 2.0 * jnp.floor(turns * 0.5 + 0.5)
    phase = -math.pi * turns
    phase_re, phase_im = jnp.cos(phase), jnp.sin(phase)
    row = lax.broadcasted_iota(jnp.int32, (LANES, LANES), 0)
    col = lax.broadcasted_iota(jnp.int32, (LANES, LANES), 1)
    angle = (2.0 * math.pi / LANES) * ((row * col) % LANES).astype(F32)
    table_re, table_im = jnp.cos(angle) * (1.0 / LENGTH), jnp.sin(angle) * (1.0 / LENGTH)
    dot = functools.partial(jnp.dot, precision=lax.Precision.HIGHEST, preferred_element_type=F32)
    line_re = dot(phase_re, table_re) - dot(phase_im, table_im)
    line_im = dot(phase_re, table_im) + dot(phase_im, table_re)
    twist = (2.0 * math.pi / LENGTH) * (q1 * q2).astype(F32)
    twist_re, twist_im = jnp.cos(twist), jnp.sin(twist)
    line_re, line_im = (
        line_re * twist_re - line_im * twist_im,
        line_re * twist_im + line_im * twist_re,
    )
    wrap = (-2.0 * math.pi / BLOCKS) * q1.astype(F32)
    wrap_re, wrap_im = jnp.cos(wrap), jnp.sin(wrap)
    line_ref[0] = line_re
    line_ref[1] = line_im
    line_ref[2] = line_re * wrap_re - line_im * wrap_im
    line_ref[3] = line_re * wrap_im + line_im * wrap_re
    ahead = col >= row

    def one(k, carry):
        def spread(part):
            line = jnp.broadcast_to(line_ref[part, pl.ds(k, 1), :], (LANES, LANES))
            return pltpu.roll(line, 0, 1, stride=1, stride_axis=0)

        re_hi, re_lo = halves(jnp.where(ahead, spread(0), spread(2)))
        im_hi, im_lo = halves(jnp.where(ahead, spread(1), spread(3)))
        for target, re, im in ((s_hi, re_hi, im_hi), (s_lo, re_lo, im_lo)):
            target[k, :LANES, :LANES] = re
            target[k, :LANES, LANES:] = im
            target[k, LANES:, :LANES] = -im
            target[k, LANES:, LANES:] = re
        return carry

    lax.fori_loop(0, BLOCKS, one, 0)


def kernel(
    fresnel_ref, slice_hbm, wave_hbm, out_hbm,
    piece, wave, trans, sent, taken, back, line_ref, s_hi, s_lo, lhs, mid, rhs, mid_row,
    slice_sem, wave_sem, z_send, z_recv, y_send, y_recv, go_send, go_recv, back_send, back_recv, answer, ready,
):
    me = lax.axis_index("rows")
    spot = lax.axis_index("dist")
    z_hi, x, core = me // 8, (me // 2) % 4, me % 2
    z_lo, y = spot // 4, spot % 4
    fetch_slice = pltpu.make_async_copy(slice_hbm, piece, slice_sem)
    fetch_slice.start()
    fetch = pltpu.make_async_copy(wave_hbm, wave, wave_sem)
    fetch.start()
    z_peers = [{"dist": (z_lo + k) % 4 * 4 + y, "rows": me} for k in (1, 3, 2)]
    y_peers = [{"dist": z_lo * 4 + (y + k) % 4, "rows": me} for k in (1, 3, 2)]
    row_peers = []
    for far, dx, other in [(f, a, c) for f in (1, 0) for a in (0, 1, 3, 2) for c in (0, 1)]:
        if (far, dx, other) != (0, 0, 0):
            row_peers.append((z_hi + far) % 2 * 8 + (x + dx) % 4 * 2 + (core + other) % 2)

    near_and_far = [p for pair in zip(row_peers[:7], row_peers[8:]) for p in pair] + row_peers[7:8]
    barrier = pltpu.get_barrier_semaphore()
    far_peers = [{"dist": spot, "rows": p} for p in row_peers[:8]]
    peers = z_peers + y_peers + [{"dist": spot, "rows": p} for p in row_peers[8:]]
    for peer in peers:
        pl.semaphore_signal(barrier, inc=1, device_id=peer)

    @pl.when(z_hi == 0)
    def _():
        for peer in far_peers:
            pl.semaphore_signal(barrier, inc=1, device_id=peer)

    fetch_slice.wait()

    def transmission(j, carry):
        rows = pl.ds(pl.multiple_of(j * SUB, SUB), SUB)
        amplitude = jnp.exp(-piece[1, rows, :])
        trans[y, z_lo, 0, rows, :] = amplitude * jnp.cos(piece[0, rows, :])
        trans[y, z_lo, 1, rows, :] = amplitude * jnp.sin(piece[0, rows, :])
        return carry

    lax.fori_loop(0, LANES // SUB, transmission, 0)
    pl.semaphore_wait(barrier, len(peers) + len(far_peers) * z_hi)

    @pl.when(z_hi == 1)
    def _():
        for peer in far_peers:
            pl.semaphore_signal(answer, inc=1, device_id=peer)

    def z_copies(g):
        own = trans.at[y, z_lo, :, pl.ds(*GO[g])]
        return [
            pltpu.make_async_remote_copy(own, own, z_send.at[g], z_recv.at[g], device_id=peer)
            for peer in z_peers
        ]

    def y_copies(g):
        own = trans.at[y, :, :, pl.ds(*GO[g])]
        return [
            pltpu.make_async_remote_copy(own, own, y_send.at[g], y_recv.at[g], device_id=peer)
            for peer in y_peers
        ]

    def settled(view, sem):
        pltpu.make_async_copy(view, view, sem).wait()

    def pass_on(g):
        settled(trans.at[0, pl.ds(0, 3), :, pl.ds(*GO[g])], z_recv.at[g])
        for copy in y_copies(g):
            copy.start()
        if g + 1 == len(GO):
            for peer in z_peers:
                pl.semaphore_signal(ready, inc=1, device_id=peer)

    def exchange(order, outbox, rows, target, send_sem, recv_sem):
        for p in order:
            pltpu.make_async_remote_copy(
                outbox.at[p, :, rows], target, send_sem, recv_sem,
                device_id={"dist": spot, "rows": p},
            ).start()
        pltpu.make_async_copy(outbox.at[me, :, rows], target, recv_sem).start()

    def column_part(first, count):
        def forward(j, carry):
            here = pl.ds(pl.multiple_of(j * SUB, SUB), SUB)
            low = pl.ds(pl.multiple_of(count + j * SUB, SUB), SUB)
            there = pl.ds(pl.multiple_of(first + j * SUB, SUB), SUB)
            points = []
            for a in range(BLOCKS):
                wave_re = wave[0, there, a * LANES : (a + 1) * LANES]
                wave_im = wave[1, there, a * LANES : (a + 1) * LANES]
                turn_re = trans[a % 4, a // 4, 0, there, :]
                turn_im = trans[a % 4, a // 4, 1, there, :]
                points.append(
                    (wave_re * turn_re - wave_im * turn_im, wave_re * turn_im + wave_im * turn_re)
                )
            for q, (re, im) in enumerate(dft16(points, -1)):
                re_hi, re_lo = halves(re)
                im_hi, im_lo = halves(im)
                lhs[q, here, :LANES] = re_hi
                lhs[q, here, LANES:] = im_hi
                lhs[q, low, :LANES] = re_lo
                lhs[q, low, LANES:] = im_lo
            return carry

        lax.fori_loop(0, count // SUB, forward, 0)

        def multiply(q, carry):
            both = jnp.dot(lhs[q, : 2 * count, :], s_hi[q], preferred_element_type=F32)
            rest = jnp.dot(lhs[q, :count, :], s_lo[q], preferred_element_type=F32)
            mid[q, :count, :] = both[:count] + (both[count:] + rest)
            return carry

        lax.fori_loop(0, BLOCKS, multiply, 0, unroll=4)

        def inverse(j, carry):
            here = pl.ds(pl.multiple_of(j * SUB, SUB), SUB)
            there = pl.ds(pl.multiple_of(first + j * SUB, SUB), SUB)
            points = [(mid[q, here, :LANES], mid[q, here, LANES:]) for q in range(BLOCKS)]
            for a, (re, im) in enumerate(dft16(points, 1)):
                sent[a, 0, there, :] = re
                sent[a, 1, there, :] = im
            return carry

        lax.fori_loop(0, count // SUB, inverse, 0)

    for g in range(len(GO)):
        for copy in z_copies(g):
            copy.start()
    build_matrices(fresnel_ref[0], line_ref, s_hi, s_lo)
    for g in range(len(GO)):
        pass_on(g)
    fetch.wait()
    for g, (first, count) in enumerate(GO):
        rows = pl.ds(first, count)
        settled(trans.at[pl.ds(0, 3), :, :, rows], y_recv.at[g])
        column_part(first, count)
        if g == 0:
            pl.semaphore_wait(ready, len(z_peers))

            @pl.when(z_hi == 0)
            def _():
                pl.semaphore_wait(answer, len(far_peers))

        exchange(near_and_far, sent, rows, taken.at[me, :, rows], go_send.at[g], go_recv.at[g])

    def row_forward(j, carry):
        here = pl.ds(pl.multiple_of(j * SUB, SUB), SUB)
        im_rows = pl.ds(pl.multiple_of(LANES + j * SUB, SUB), SUB)
        points = [(taken[a, 0, here, :], taken[a, 1, here, :]) for a in range(BLOCKS)]
        for q, (re, im) in enumerate(dft16(points, -1)):
            re_hi, re_lo = halves(re)
            im_hi, im_lo = halves(-im)
            rhs[q, here, :LANES] = re_hi
            rhs[q, here, LANES:] = re_lo
            rhs[q, im_rows, :LANES] = im_hi
            rhs[q, im_rows, LANES:] = im_lo
        return carry

    for g, (first, count) in enumerate(GO):
        settled(taken.at[:, :, pl.ds(first, count)], go_recv.at[g])
        lax.fori_loop(first // SUB, (first + count) // SUB, row_forward, 0)

    def row_multiply(q, carry):
        turn = (BLOCKS - q) % BLOCKS
        both = jnp.dot(s_hi[turn], rhs[q], preferred_element_type=F32)
        rest = jnp.dot(s_lo[turn], rhs[q, :, :LANES], preferred_element_type=F32)
        mid_row[q] = both[:, :LANES] + (both[:, LANES:] + rest)
        return carry

    lax.fori_loop(0, BLOCKS, row_multiply, 0, unroll=16)

    def row_inverse(j, carry):
        here = pl.ds(pl.multiple_of(j * SUB, SUB), SUB)
        im_rows = pl.ds(pl.multiple_of(LANES + j * SUB, SUB), SUB)
        points = [(mid_row[q, here, :], -mid_row[q, im_rows, :]) for q in range(BLOCKS)]
        for a, (re, im) in enumerate(dft16(points, 1)):
            back[a, 0, here, :] = re
            back[a, 1, here, :] = im
        return carry

    cols = pl.ds(pl.multiple_of(me * LANES, LANES), LANES)
    for g, (first, count) in enumerate(BACK):
        lax.fori_loop(first // SUB, (first + count) // SUB, row_inverse, 0)
        rows = pl.ds(first, count)
        exchange(row_peers, back, rows, out_hbm.at[:, rows, cols], back_send.at[g], back_recv)

    for g, (first, count) in enumerate(GO):
        for copy in z_copies(g) + y_copies(g):
            copy.wait_send()
        settled(sent.at[pl.ds(0, BLOCKS - 1), :, pl.ds(first, count)], go_send.at[g])
    for g, (first, count) in enumerate(BACK):
        settled(back.at[pl.ds(0, BLOCKS - 1), :, pl.ds(first, count)], back_send.at[g])
    settled(out_hbm, back_recv)


def body(wave, object_slice, fresnel):
    box = pltpu.VMEM((BLOCKS, 2, LANES, LANES), F32)
    matrices = pltpu.VMEM((BLOCKS, 2 * LANES, 2 * LANES), BF16)
    most = max(count for _, count in GO)
    dma = pltpu.SemaphoreType.DMA
    go = dma((len(GO),))
    out = pl.pallas_call(
        kernel,
        out_shape=jax.ShapeDtypeStruct((2, LANES, LENGTH), F32),
        in_specs=[
            pl.BlockSpec(memory_space=pltpu.SMEM),
            pl.BlockSpec(memory_space=pl.ANY),
            pl.BlockSpec(memory_space=pl.ANY),
        ],
        out_specs=pl.BlockSpec(memory_space=pl.ANY),
        scratch_shapes=[
            pltpu.VMEM((2, LANES, LANES), F32),
            pltpu.VMEM((2, LANES, LENGTH), F32),
            pltpu.VMEM((4, 4, 2, LANES, LANES), F32),
            box, box, box,
            pltpu.VMEM((4, BLOCKS, LANES), F32),
            matrices, matrices,
            pltpu.VMEM((BLOCKS, 2 * most, 2 * LANES), BF16),
            pltpu.VMEM((BLOCKS, most, 2 * LANES), F32),
            matrices,
            pltpu.VMEM((BLOCKS, 2 * LANES, LANES), F32),
            dma, dma, go, go, go, go, go, go, dma((len(BACK),)), dma,
            pltpu.SemaphoreType.REGULAR, pltpu.SemaphoreType.REGULAR,
        ],
        compiler_params=pltpu.CompilerParams(
            collective_id=0, has_side_effects=True, vmem_limit_bytes=50 << 20
        ),
        name="propagate",
    )(fresnel, *(pltpu.with_memory_space_constraint(a, pltpu.HBM) for a in (object_slice, wave[0])))
    return out[None]


def solution(mesh):
    return jax.shard_map(
        body,
        mesh=mesh,
        in_specs=(P("dist", None, "rows", None), P(None, "rows", "dist"), P("dist")),
        out_specs=P("dist", None, "rows", None),
        check_vma=False,
    )
```

```python
import functools
import math

import jax
import jax.numpy as jnp
from jax import lax
from jax.experimental import pallas as pl
from jax.experimental.pallas import tpu as pltpu
from jax.sharding import PartitionSpec as P

F32 = jnp.float32
BF16 = jnp.bfloat16
LANES = 128
BLOCKS = 16
LENGTH = LANES * BLOCKS
SUB = 16
GO = ((0, 32), (32, 32), (64, 64),)
BACK = ((0, 32), (32, 32), (64, 64),)


def dft4(points, direction):
    (ar, ai), (br, bi), (cr, ci), (dr, di) = points
    er, ei, fr, fi = ar + cr, ai + ci, ar - cr, ai - ci
    gr, gi, hr, hi = br + dr, bi + di, br - dr, bi - di
    plus, minus = (fr - hi, fi + hr), (fr + hi, fi - hr)
    if direction < 0:
        plus, minus = minus, plus
    return [(er + gr, ei + gi), plus, (er - gr, ei - gi), minus]


def turned(point, steps, direction):
    re, im = point
    steps %= 16
    if steps == 0:
        return point
    if steps == 4:
        return (-im, re) if direction > 0 else (im, -re)
    angle = direction * 2.0 * math.pi * steps / 16
    turn_re, turn_im = math.cos(angle), math.sin(angle)
    if steps == 2:
        return ((re - direction * im) * turn_re, (im + direction * re) * turn_re)
    return (re * turn_re - im * turn_im, re * turn_im + im * turn_re)


def dft16(points, direction):
    inner = [dft4([points[4 * a1 + a0] for a1 in range(4)], direction) for a0 in range(4)]
    out = [None] * 16
    for q0 in range(4):
        column = [turned(inner[a0][q0], a0 * q0, direction) for a0 in range(4)]
        for q1, value in enumerate(dft4(column, direction)):
            out[q0 + 4 * q1] = value
    return out


def halves(value):
    high = value.astype(BF16)
    return high, (value - high.astype(F32)).astype(BF16)


def build_matrices(fresnel, line_ref, s_hi, s_lo):
    q1 = lax.broadcasted_iota(jnp.int32, (BLOCKS, LANES), 0)
    q2 = lax.broadcasted_iota(jnp.int32, (BLOCKS, LANES), 1)
    index = q1 + BLOCKS * q2
    signed = jnp.where(index < LENGTH // 2, index, index - LENGTH).astype(F32)
    turns = fresnel * (signed * signed) * (1.0 / (LENGTH * LENGTH))
    turns = turns - 2.0 * jnp.floor(turns * 0.5 + 0.5)
    phase = -math.pi * turns
    phase_re, phase_im = jnp.cos(phase), jnp.sin(phase)
    row = lax.broadcasted_iota(jnp.int32, (LANES, LANES), 0)
    col = lax.broadcasted_iota(jnp.int32, (LANES, LANES), 1)
    angle = (2.0 * math.pi / LANES) * ((row * col) % LANES).astype(F32)
    table_re, table_im = jnp.cos(angle) * (1.0 / LENGTH), jnp.sin(angle) * (1.0 / LENGTH)
    dot = functools.partial(jnp.dot, precision=lax.Precision.HIGHEST, preferred_element_type=F32)
    line_re = dot(phase_re, table_re) - dot(phase_im, table_im)
    line_im = dot(phase_re, table_im) + dot(phase_im, table_re)
    twist = (2.0 * math.pi / LENGTH) * (q1 * q2).astype(F32)
    twist_re, twist_im = jnp.cos(twist), jnp.sin(twist)
    line_re, line_im = (
        line_re * twist_re - line_im * twist_im,
        line_re * twist_im + line_im * twist_re,
    )
    wrap = (-2.0 * math.pi / BLOCKS) * q1.astype(F32)
    wrap_re, wrap_im = jnp.cos(wrap), jnp.sin(wrap)
    line_ref[0] = line_re
    line_ref[1] = line_im
    line_ref[2] = line_re * wrap_re - line_im * wrap_im
    line_ref[3] = line_re * wrap_im + line_im * wrap_re
    ahead = col >= row

    def one(k, carry):
        def spread(part):
            line = jnp.broadcast_to(line_ref[part, pl.ds(k, 1), :], (LANES, LANES))
            return pltpu.roll(line, 0, 1, stride=1, stride_axis=0)

        re_hi, re_lo = halves(jnp.where(ahead, spread(0), spread(2)))
        im_hi, im_lo = halves(jnp.where(ahead, spread(1), spread(3)))
        for target, re, im in ((s_hi, re_hi, im_hi), (s_lo, re_lo, im_lo)):
            target[k, :LANES, :LANES] = re
            target[k, :LANES, LANES:] = im
            target[k, LANES:, :LANES] = -im
            target[k, LANES:, LANES:] = re
        return carry

    lax.fori_loop(0, BLOCKS, one, 0)


def kernel(
    fresnel_ref, slice_hbm, wave_hbm, out_hbm,
    piece, wave, trans, sent, taken, back, line_ref, s_hi, s_lo, lhs, mid, rhs, mid_row,
    slice_sem, wave_sem, z_send, z_recv, y_send, y_recv, go_send, go_recv, back_send, back_recv, answer, ready,
):
    me = lax.axis_index("rows")
    spot = lax.axis_index("dist")
    z_hi, x, core = me // 8, (me // 2) % 4, me % 2
    z_lo, y = spot // 4, spot % 4
    fetch_slice = pltpu.make_async_copy(slice_hbm, piece, slice_sem)
    fetch_slice.start()
    fetch = pltpu.make_async_copy(wave_hbm, wave, wave_sem)
    fetch.start()
    z_peers = [{"dist": (z_lo + k) % 4 * 4 + y, "rows": me} for k in (1, 3, 2)]
    y_peers = [{"dist": z_lo * 4 + (y + k) % 4, "rows": me} for k in (1, 3, 2)]
    row_peers = []
    for far, dx, other in [(f, a, c) for f in (1, 0) for a in (0, 1, 3, 2) for c in (0, 1)]:
        if (far, dx, other) != (0, 0, 0):
            row_peers.append((z_hi + far) % 2 * 8 + (x + dx) % 4 * 2 + (core + other) % 2)

    near_and_far = [p for pair in zip(row_peers[:7], row_peers[8:]) for p in pair] + row_peers[7:8]
    barrier = pltpu.get_barrier_semaphore()
    far_peers = [{"dist": spot, "rows": p} for p in row_peers[:8]]
    peers = z_peers + y_peers + [{"dist": spot, "rows": p} for p in row_peers[8:]]
    for peer in peers:
        pl.semaphore_signal(barrier, inc=1, device_id=peer)

    @pl.when(z_hi == 0)
    def _():
        for peer in far_peers:
            pl.semaphore_signal(barrier, inc=1, device_id=peer)

    fetch_slice.wait()

    def transmission(j, carry):
        rows = pl.ds(pl.multiple_of(j * SUB, SUB), SUB)
        amplitude = jnp.exp(-piece[1, rows, :])
        trans[y, z_lo, 0, rows, :] = amplitude * jnp.cos(piece[0, rows, :])
        trans[y, z_lo, 1, rows, :] = amplitude * jnp.sin(piece[0, rows, :])
        return carry

    lax.fori_loop(0, LANES // SUB, transmission, 0)
    pl.semaphore_wait(barrier, len(peers) + len(far_peers) * z_hi)

    @pl.when(z_hi == 1)
    def _():
        for peer in far_peers:
            pl.semaphore_signal(answer, inc=1, device_id=peer)

    def z_copies(g):
        own = trans.at[y, z_lo, :, pl.ds(*GO[g])]
        return [
            pltpu.make_async_remote_copy(own, own, z_send.at[g], z_recv.at[g], device_id=peer)
            for peer in z_peers
        ]

    def y_copies(g):
        own = trans.at[y, :, :, pl.ds(*GO[g])]
        return [
            pltpu.make_async_remote_copy(own, own, y_send.at[g], y_recv.at[g], device_id=peer)
            for peer in y_peers
        ]

    def settled(view, sem):
        pltpu.make_async_copy(view, view, sem).wait()

    def pass_on(g):
        settled(trans.at[0, pl.ds(0, 3), :, pl.ds(*GO[g])], z_recv.at[g])
        for copy in y_copies(g):
            copy.start()
        if g + 1 == len(GO):
            for peer in z_peers:
                pl.semaphore_signal(ready, inc=1, device_id=peer)

    def exchange(order, outbox, rows, target, send_sem, recv_sem):
        for p in order:
            pltpu.make_async_remote_copy(
                outbox.at[p, :, rows], target, send_sem, recv_sem,
                device_id={"dist": spot, "rows": p},
            ).start()
        pltpu.make_async_copy(outbox.at[me, :, rows], target, recv_sem).start()

    def column_part(first, count):
        def forward(j, carry):
            here = pl.ds(pl.multiple_of(j * SUB, SUB), SUB)
            low = pl.ds(pl.multiple_of(count + j * SUB, SUB), SUB)
            there = pl.ds(pl.multiple_of(first + j * SUB, SUB), SUB)
            points = []
            for a in range(BLOCKS):
                wave_re = wave[0, there, a * LANES : (a + 1) * LANES]
                wave_im = wave[1, there, a * LANES : (a + 1) * LANES]
                turn_re = trans[a % 4, a // 4, 0, there, :]
                turn_im = trans[a % 4, a // 4, 1, there, :]
                points.append(
                    (wave_re * turn_re - wave_im * turn_im, wave_re * turn_im + wave_im * turn_re)
                )
            for q, (re, im) in enumerate(dft16(points, -1)):
                re_hi, re_lo = halves(re)
                im_hi, im_lo = halves(im)
                lhs[q, here, :LANES] = re_hi
                lhs[q, here, LANES:] = im_hi
                lhs[q, low, :LANES] = re_lo
                lhs[q, low, LANES:] = im_lo
            return carry

        lax.fori_loop(0, count // SUB, forward, 0)

        def multiply(q, carry):
            both = jnp.dot(lhs[q, : 2 * count, :], s_hi[q], preferred_element_type=F32)
            rest = jnp.dot(lhs[q, :count, :], s_lo[q], preferred_element_type=F32)
            mid[q, :count, :] = both[:count] + (both[count:] + rest)
            return carry

        lax.fori_loop(0, BLOCKS, multiply, 0, unroll=8)

        def inverse(j, carry):
            here = pl.ds(pl.multiple_of(j * SUB, SUB), SUB)
            there = pl.ds(pl.multiple_of(first + j * SUB, SUB), SUB)
            points = [(mid[q, here, :LANES], mid[q, here, LANES:]) for q in range(BLOCKS)]
            for a, (re, im) in enumerate(dft16(points, 1)):
                sent[a, 0, there, :] = re
                sent[a, 1, there, :] = im
            return carry

        lax.fori_loop(0, count // SUB, inverse, 0)

    for g in range(len(GO)):
        for copy in z_copies(g):
            copy.start()
    build_matrices(fresnel_ref[0], line_ref, s_hi, s_lo)
    for g in range(len(GO)):
        pass_on(g)
    fetch.wait()
    for g, (first, count) in enumerate(GO):
        rows = pl.ds(first, count)
        settled(trans.at[pl.ds(0, 3), :, :, rows], y_recv.at[g])
        column_part(first, count)
        if g == 0:
            pl.semaphore_wait(ready, len(z_peers))

            @pl.when(z_hi == 0)
            def _():
                pl.semaphore_wait(answer, len(far_peers))

        exchange(near_and_far, sent, rows, taken.at[me, :, rows], go_send.at[g], go_recv.at[g])

    def row_forward(j, carry):
        here = pl.ds(pl.multiple_of(j * SUB, SUB), SUB)
        im_rows = pl.ds(pl.multiple_of(LANES + j * SUB, SUB), SUB)
        points = [(taken[a, 0, here, :], taken[a, 1, here, :]) for a in range(BLOCKS)]
        for q, (re, im) in enumerate(dft16(points, -1)):
            re_hi, re_lo = halves(re)
            im_hi, im_lo = halves(-im)
            rhs[q, here, :LANES] = re_hi
            rhs[q, here, LANES:] = re_lo
            rhs[q, im_rows, :LANES] = im_hi
            rhs[q, im_rows, LANES:] = im_lo
        return carry

    for g, (first, count) in enumerate(GO):
        settled(taken.at[:, :, pl.ds(first, count)], go_recv.at[g])
        lax.fori_loop(first // SUB, (first + count) // SUB, row_forward, 0)

    def row_multiply(q, carry):
        turn = (BLOCKS - q) % BLOCKS
        both = jnp.dot(s_hi[turn], rhs[q], preferred_element_type=F32)
        rest = jnp.dot(s_lo[turn], rhs[q, :, :LANES], preferred_element_type=F32)
        mid_row[q] = both[:, :LANES] + (both[:, LANES:] + rest)
        return carry

    lax.fori_loop(0, BLOCKS, row_multiply, 0, unroll=16)

    def row_inverse(j, carry):
        here = pl.ds(pl.multiple_of(j * SUB, SUB), SUB)
        im_rows = pl.ds(pl.multiple_of(LANES + j * SUB, SUB), SUB)
        points = [(mid_row[q, here, :], -mid_row[q, im_rows, :]) for q in range(BLOCKS)]
        for a, (re, im) in enumerate(dft16(points, 1)):
            back[a, 0, here, :] = re
            back[a, 1, here, :] = im
        return carry

    cols = pl.ds(pl.multiple_of(me * LANES, LANES), LANES)
    for g, (first, count) in enumerate(BACK):
        lax.fori_loop(first // SUB, (first + count) // SUB, row_inverse, 0)
        rows = pl.ds(first, count)
        exchange(row_peers, back, rows, out_hbm.at[:, rows, cols], back_send.at[g], back_recv)

    for g, (first, count) in enumerate(GO):
        for copy in z_copies(g) + y_copies(g):
            copy.wait_send()
        settled(sent.at[pl.ds(0, BLOCKS - 1), :, pl.ds(first, count)], go_send.at[g])
    for g, (first, count) in enumerate(BACK):
        settled(back.at[pl.ds(0, BLOCKS - 1), :, pl.ds(first, count)], back_send.at[g])
    settled(out_hbm, back_recv)


def body(wave, object_slice, fresnel):
    box = pltpu.VMEM((BLOCKS, 2, LANES, LANES), F32)
    matrices = pltpu.VMEM((BLOCKS, 2 * LANES, 2 * LANES), BF16)
    most = max(count for _, count in GO)
    dma = pltpu.SemaphoreType.DMA
    go = dma((len(GO),))
    out = pl.pallas_call(
        kernel,
        out_shape=jax.ShapeDtypeStruct((2, LANES, LENGTH), F32),
        in_specs=[
            pl.BlockSpec(memory_space=pltpu.SMEM),
            pl.BlockSpec(memory_space=pl.ANY),
            pl.BlockSpec(memory_space=pl.ANY),
        ],
        out_specs=pl.BlockSpec(memory_space=pl.ANY),
        scratch_shapes=[
            pltpu.VMEM((2, LANES, LANES), F32),
            pltpu.VMEM((2, LANES, LENGTH), F32),
            pltpu.VMEM((4, 4, 2, LANES, LANES), F32),
            box, box, box,
            pltpu.VMEM((4, BLOCKS, LANES), F32),
            matrices, matrices,
            pltpu.VMEM((BLOCKS, 2 * most, 2 * LANES), BF16),
            pltpu.VMEM((BLOCKS, most, 2 * LANES), F32),
            matrices,
            pltpu.VMEM((BLOCKS, 2 * LANES, LANES), F32),
            dma, dma, go, go, go, go, go, go, dma((len(BACK),)), dma,
            pltpu.SemaphoreType.REGULAR, pltpu.SemaphoreType.REGULAR,
        ],
        compiler_params=pltpu.CompilerParams(
            collective_id=0, has_side_effects=True, vmem_limit_bytes=50 << 20
        ),
        name="propagate",
    )(fresnel, *(pltpu.with_memory_space_constraint(a, pltpu.HBM) for a in (object_slice, wave[0])))
    return out[None]


def solution(mesh):
    return jax.shard_map(
        body,
        mesh=mesh,
        in_specs=(P("dist", None, "rows", None), P(None, "rows", "dist"), P("dist")),
        out_specs=P("dist", None, "rows", None),
        check_vma=False,
    )
```
